256 devices in a mesh: dp: 4 (over x), mp: 64 (over z, y, core).
Axes of the slice: x: 4, y: 4, z: 8, core: 2. Of those that a mesh axis runs over, the one named last changes fastest.
Arguments:
- tokens: bfloat16 [4096, 2048], P('dp'), may hold values from -6 to 6
- domain_ids: int32 [4096], P('dp'), may hold values from 0 to 21
- domain_bias: bfloat16 [22, 2048], replicated, may hold values from -3 to 3
- dense_gate: bfloat16 [2048, 10944], P(None, 'mp'), may hold values from -0.125 to 0.125
- dense_up: bfloat16 [2048, 10944], P(None, 'mp'), may hold values from -0.125 to 0.125
- dense_down: bfloat16 [10944, 2048], P('mp'), may hold values from -0.0546875 to 0.0546875
- shared_gate: bfloat16 [2048, 2816], P(None, 'mp'), may hold values from -0.125 to 0.125
- shared_up: bfloat16 [2048, 2816], P(None, 'mp'), may hold values from -0.125 to 0.125
- shared_down: bfloat16 [2816, 2048], P('mp'), may hold values from -0.109375 to 0.109375
- expert_gate: bfloat16 [64, 2048, 1408], P('mp', None, 'dp'), may hold values from -0.125 to 0.125
- expert_up: bfloat16 [64, 2048, 1408], P('mp', None, 'dp'), may hold values from -0.125 to 0.125
- expert_down: bfloat16 [64, 1408, 2048], P('mp', 'dp'), may hold values from -0.15625 to 0.15625
- expert_ids: int32 [4096, 6], P('dp'), may hold values from 0 to 63, all different within a row; in each aligned block of 16 rows (0 to 15, 16 to 31, ...) at most 3 rows name the same one
- route_weights: float32 [4096, 6], P('dp'), may hold values from 0.05 to 0.6
Outputs:
- mixed: bfloat16 [4096, 2048], P(('dp', 'mp'))
The draws below stay inside these ranges and needn't reach their ends.
Inputs may be any that keep to these rules, and one draw needn't show every extreme that they name: `expert_ids`: each row names 6 different experts; in the 16 rows of one device (aligned blocks in order) no expert is named more than 3 times, and in some blocks one expert exactly 3 times.
All inputs are finite; a program needn't handle non-finite values.
Results may differ from the reference program's by a relative error of at most 0.009.
Values may be sent and summed in bfloat16 or wider, within the bound.
No kernel may reach another device: no remote copies, remote signals or barrier semaphores. Data moves between devices by JAX's collectives and lax.ppermute only.
A program may use at most 128 MiB of HBM per device.

```python
import math
import jax
import jax.numpy as jnp
import numpy as np
from jax import lax

D = 2048
FF = 10944
SH = 2816
EH = 1408
TOP = 6
DOMAINS = 22
TOK_DEV = 16
EXPERTS = 64
TOKENS = 4096
MOST = 3
N_DP = 4
N_MP = 64


def set_ends(array, rng, least, high):
    longest = array.shape.index(max(array.shape))
    spots = []
    for shift in (0, 1):
        where = [jax.random.randint(jax.random.fold_in(rng, axis), (), 0, length) for axis, length in enumerate(array.shape)]
        where[longest] = (where[longest] + shift) % array.shape[longest]
        spots.append(tuple(where))
    return array.at[spots[0]].set(least).at[spots[1]].set(high)


def block_levels(stream_key, dims, split, least, top_value):
    gain, own = 1.0, jax.random.fold_in(stream_key, 6)
    for dim, blocks in split:
        heights = jnp.exp(jax.random.uniform(jax.random.fold_in(own, dim), (blocks,), jnp.float32, least / len(split), top_value / len(split)))
        gain = gain * jnp.repeat(heights, dims[dim] // blocks).reshape([-1 if axis == dim else 1 for axis in range(len(dims))])
    return gain


def rank_bounds(number_of, skew):
    portions = [(1 << 20) // math.isqrt(grade ** skew) + 1 for grade in range(1, number_of + 1)]
    width = 1 + sum(portions) // (1 << 30)
    return np.cumsum(np.array([max(1, weight // width) for weight in portions]))


def ranked_ids(stream_key, dims, count, skew):
    table = rank_bounds(count, skew)
    pick = jax.random.randint(jax.random.fold_in(stream_key, 1), dims, 0, int(table[count - 1]))
    standing = jnp.searchsorted(jnp.asarray(table, jnp.int32), pick, side="right")
    return jax.random.permutation(jax.random.fold_in(stream_key, 2), count)[standing].astype(jnp.int32)


def deal_out(key, own, number, rows, amount, top, limit, lean):
    ranking = jax.random.permutation(key, amount)
    crowded, ordinary = portions_of(amount, rows * top, limit, lean, True), portions_of(amount, rows * top, limit, lean, False)
    places = jnp.arange(amount)

    def named(sizes, rotation):
        used = int((sizes > 0).sum())
        fixed = max(1, used // 4)
        passed = fixed + (places - fixed + rotation * (used - fixed)) % max(1, amount - fixed)
        return jnp.zeros((amount,), jnp.int32).at[ranking[jnp.where(places < fixed, places, passed)]].set(jnp.asarray(sizes, jnp.int32))

    sizes = jnp.where(number % 4 == 0, named(crowded, number // 4), named(ordinary, number - number // 4 - 1))
    mixed = jax.random.permutation(jax.random.fold_in(own, 3), amount)
    source_of, receiver = mixed[0:amount // 2 * 2:2], mixed[1:amount // 2 * 2:2]
    room = jnp.minimum(sizes[source_of] - 1, limit - sizes[receiver]) // 2
    room = jnp.where((source_of == ranking[0]) | (receiver == ranking[0]) | (sizes[receiver] == 0), 0, jnp.maximum(room, 0))
    passed = jax.random.randint(jax.random.fold_in(own, 4), (amount // 2,), 0, 1 << 20) % (room + 1)
    sizes = sizes.at[source_of].add(-passed).at[receiver].add(passed)
    items = jnp.searchsorted(jnp.cumsum(sizes), jnp.arange(rows * top), side="right").astype(jnp.int32)
    listing = items.reshape(top, rows).T
    listing = listing[jax.random.permutation(jax.random.fold_in(own, 1), rows)]
    rotation = jax.random.randint(jax.random.fold_in(own, 2), (rows, 1), 0, top)
    return jnp.take_along_axis(listing, (jnp.arange(top)[None, :] + rotation) % top, axis=1)


def portions_of(number_of, total, most, lean, full):
    weights = [(1 << 20) // math.isqrt(rank ** lean) + 1 for rank in range(1, number_of + 1)]
    largest = most if full else min(most, max(-(-total // number_of), total * weights[0] // sum(weights)))
    least = 1 if total - largest >= number_of - 1 else 0
    given, spare = [largest] + [least] * (number_of - 1), total - largest - least * (number_of - 1)
    while spare > 0:
        free = [i for i in range(1, number_of) if given[i] < largest] or [i for i in range(1, number_of) if given[i] < most]
        mass, left = sum([weights[i] for i in free]), spare
        for i in free:
            more = min(most - given[i], max(1, left * weights[i] // mass), spare)
            given[i] = given[i] + more
            spare = spare - more
    return np.array(given)


def normal_values(rng, dims, width, reach, pieces=(), held_as=jnp.bfloat16):
    drawn = jax.random.normal(rng, dims, jnp.float32) * width
    if len(pieces) > 0:
        drawn = block_levels(rng, dims, pieces, -0.22, 0.18) * drawn
    return jnp.clip(drawn, min=-reach, max=reach).astype(held_as)


def setup_inputs(seed: int = 0) -> dict:
    key_of = jax.random.split(jax.random.key(seed), 15)
    tokens = normal_values(key_of[0], (TOKENS, D), 1.0, 6.0, ((0, 4),))
    domain_ids = set_ends(ranked_ids(key_of[1], (TOKENS,), DOMAINS, 2), jax.random.fold_in(key_of[1], 3), 0, DOMAINS - 1).astype(jnp.int32)
    domain_bias = normal_values(key_of[2], (DOMAINS, D), 0.5, 3.0)
    dense_gate = normal_values(key_of[3], (D, FF), D ** -0.5, 0.125, ((1, 64),))
    dense_up = normal_values(key_of[4], (D, FF), D ** -0.5, 0.125, ((1, 64),))
    dense_down = normal_values(key_of[5], (FF, D), FF ** -0.5, 0.0546875, ((0, 64),))
    shared_gate = normal_values(key_of[6], (D, SH), D ** -0.5, 0.125, ((1, 64),))
    shared_up = normal_values(key_of[7], (D, SH), D ** -0.5, 0.125, ((1, 64),))
    shared_down = normal_values(key_of[8], (SH, D), SH ** -0.5, 0.109375, ((0, 64),))
    expert_gate = normal_values(key_of[9], (EXPERTS, D, EH), D ** -0.5, 0.125, ((0, 64), (2, 4)))
    expert_up = normal_values(key_of[10], (EXPERTS, D, EH), D ** -0.5, 0.125, ((0, 64), (2, 4)))
    expert_down = normal_values(key_of[11], (EXPERTS, EH, D), EH ** -0.5, 0.15625, ((0, 64), (1, 4)))
    expert_ids_keys = jax.random.split(jax.random.fold_in(key_of[12], 1), TOKENS // TOK_DEV)
    expert_ids_turns = jax.random.permutation(jax.random.fold_in(key_of[12], 3), TOKENS // TOK_DEV)
    expert_ids = jax.vmap(lambda own, number: deal_out(jax.random.fold_in(key_of[12], 2), own, number, TOK_DEV, EXPERTS, TOP, MOST, 2))(expert_ids_keys, expert_ids_turns).reshape((TOKENS, TOP))
    route_weights = jnp.clip(jnp.exp(math.log(0.6) - 2.4849067 * jax.random.uniform(key_of[13], (TOKENS, TOP), jnp.float32) ** block_levels(key_of[13], (TOKENS, TOP), ((0, 4),), -0.2, 0.2)), 0.05, 0.6)
    return dict(tokens=tokens, domain_ids=domain_ids, domain_bias=domain_bias, dense_gate=dense_gate, dense_up=dense_up, dense_down=dense_down, shared_gate=shared_gate, shared_up=shared_up, shared_down=shared_down, expert_gate=expert_gate, expert_up=expert_up, expert_down=expert_down, expert_ids=expert_ids, route_weights=route_weights)


def swiglu(rows, w_gate, w_up):
    gate = jnp.dot(rows, w_gate, preferred_element_type=jnp.float32)
    up = jnp.dot(rows, w_up, preferred_element_type=jnp.float32)
    return (jax.nn.silu(gate) * up).astype(jnp.bfloat16)


def reference(tokens, domain_ids, domain_bias, dense_gate, dense_up, dense_down, shared_gate, shared_up, shared_down, expert_gate, expert_up, expert_down, expert_ids, route_weights):
    stream = (tokens.astype(jnp.float32) + domain_bias.astype(jnp.float32)[domain_ids]).astype(jnp.bfloat16)
    dense_hidden = swiglu(stream, dense_gate, dense_up)
    resid = (stream.astype(jnp.float32) + jnp.dot(dense_hidden, dense_down, preferred_element_type=jnp.float32)).astype(jnp.bfloat16)
    shared_hidden = swiglu(resid, shared_gate, shared_up)
    shared_out = jnp.dot(shared_hidden, shared_down, preferred_element_type=jnp.float32)
    capacity = N_DP * N_MP * MOST

    def one_expert(carry, inputs):
        expert, w_gate, w_up, w_down = inputs
        hit = expert_ids == expert
        chosen = jnp.any(hit, axis=1)
        weight = jnp.sum(jnp.where(hit, route_weights, 0.0), axis=1)
        order = jnp.argsort(jnp.where(chosen, 0, 1).astype(jnp.int32), stable=True)[:capacity].astype(jnp.int32)
        hidden = swiglu(resid[order], w_gate, w_up)
        outputs = jnp.dot(hidden, w_down, preferred_element_type=jnp.float32).astype(jnp.bfloat16)
        coef = jnp.where(chosen[order], weight[order], 0.0)
        carry = carry.at[order].add(coef[:, None] * outputs.astype(jnp.float32))
        return carry, None

    start = jnp.zeros(resid.shape, jnp.float32)
    experts = jnp.arange(expert_gate.shape[0], dtype=jnp.int32)
    routed, _ = lax.scan(one_expert, start, (experts, expert_gate, expert_up, expert_down))
    return (resid.astype(jnp.float32) + shared_out + routed).astype(jnp.bfloat16)
```

```python
import jax
import jax.numpy as jnp
from jax import lax
from jax.sharding import PartitionSpec as P

BF = jnp.bfloat16
F32 = jnp.float32
NX, NZ, NY = 4, 8, 4
NB = NZ * NY


def mp_perm(dz, dy, dc):
    pairs = []
    for z in range(NZ):
        for y in range(NY):
            for c in range(2):
                to = ((z + dz) % NZ) * 2 * NY + ((y + dy) % NY) * 2 + (c + dc) % 2
                pairs.append((z * 2 * NY + y * 2 + c, to))
    return pairs


def core_swap(v):
    return lax.ppermute(v, "mp", mp_perm(0, 0, 1))


def z_shift(v, s):
    return lax.ppermute(v, "mp", mp_perm(s, 0, 0))


def y_shift(v, s):
    return lax.ppermute(v, "mp", mp_perm(0, s, 0))


def x_shift(v, s):
    return lax.ppermute(v, "dp", [(i, (i + s) % NX) for i in range(NX)])


def ring4_reduce(lo, hi, shift):
    a = shift(lo[2], 1)
    b = shift(hi[2], -1)
    c = shift(hi[1], 1)
    d = shift(lo[3], -1)
    e = shift((lo[1].astype(F32) + a.astype(F32)).astype(BF), 1)
    f = shift((hi[3].astype(F32) + b.astype(F32)).astype(BF), -1)
    own_lo = lo[0].astype(F32) + d.astype(F32) + e.astype(F32)
    own_hi = hi[0].astype(F32) + c.astype(F32) + f.astype(F32)
    return own_lo, own_hi


def ring4_gather(lo, hi, shift):
    a = shift(lo, 1)
    b = shift(hi, -1)
    c = shift(hi, 1)
    d = shift(lo, -1)
    e = shift(a, 1)
    f = shift(b, -1)
    return [lo, d, e, a], [hi, b, f, c]


def z_reduce(part):
    total = part[0].astype(F32)
    for s in (4, 3, 5, 2, 6, 1, 7):
        total = total + z_shift(part[s], s).astype(F32)
    return total


def z_gather(own):
    got = [own] + [None] * 7
    for s in (4, 3, 5, 2, 6, 1, 7):
        got[NZ - s] = z_shift(own, s)
    return jnp.concatenate(got, axis=0)


def dot(a, b):
    return jnp.dot(a, b, preferred_element_type=F32)


def swiglu(rows, w_gate, w_up):
    gate = dot(rows, w_gate)
    up = dot(rows, w_up)
    return (jax.nn.silu(gate) * up).astype(BF)


def reduce_rows(part):
    n = part.shape[1]
    half = NZ // 2 * 16
    lo = [part[d * 128 : d * 128 + half] for d in range(NY)]
    hi = [part[d * 128 + half : (d + 1) * 128] for d in range(NY)]
    own_lo, own_hi = ring4_reduce(lo, hi, y_shift)
    mid = jnp.concatenate([own_lo, own_hi], axis=0).astype(BF)
    return z_reduce(mid.reshape(NZ, 16, n))


def gather_rows(own):
    block = z_gather(own)
    half = NZ // 2 * 16
    los, his = ring4_gather(block[:half], block[half:], y_shift)
    return jnp.concatenate([v for pair in zip(los, his) for v in pair], axis=0)


def body(
    tokens,
    domain_ids,
    domain_bias,
    dense_gate,
    dense_up,
    dense_down,
    shared_gate,
    shared_up,
    shared_down,
    expert_gate,
    expert_up,
    expert_down,
    expert_ids,
    route_weights,
):
    column = lax.axis_index("mp")
    z, y, c = column // (2 * NY), (column // 2) % NY, column % 2
    d_model = tokens.shape[1]
    dy = jnp.arange(NY, dtype=jnp.int32)[:, None]
    dz = jnp.arange(NZ, dtype=jnp.int32)[None, :]
    blocks = (((z + dz) % NZ) * 2 * NY + ((y + dy) % NY) * 2 + c).reshape(NB)
    rows = NB * 16

    other_dense = [core_swap(w) for w in (dense_gate, dense_up, dense_down)]

    my_tokens = jnp.take(tokens.reshape(2 * NB, 16, d_model), blocks, axis=0).reshape(rows, d_model)
    my_domains = jnp.take(domain_ids.reshape(2 * NB, 16), blocks, axis=0).reshape(rows)
    my_ids = jnp.take(expert_ids.reshape(2 * NB, 16, -1), blocks, axis=0)
    my_weights = jnp.take(route_weights.reshape(2 * NB, 16, -1), blocks, axis=0)

    lookup = (my_domains[:, None] == jnp.arange(domain_bias.shape[0], dtype=jnp.int32)[None, :]).astype(BF)
    stream = (my_tokens.astype(F32) + dot(lookup, domain_bias)).astype(BF)

    held = (shared_gate, shared_up, shared_down, expert_gate[0], expert_up[0], expert_down[0])
    held, other_dense = lax.optimization_barrier((held, other_dense))
    other_held = [core_swap(w) for w in held]

    hidden = swiglu(stream, dense_gate, dense_up)
    other_hidden = swiglu(stream, other_dense[0], other_dense[1])
    partial = (dot(hidden, dense_down) + dot(other_hidden, other_dense[2])).astype(BF)
    total = reduce_rows(partial)
    own_resid = (stream[:16].astype(F32) + total).astype(BF)
    resid = gather_rows(own_resid)

    most = 3
    spots, weights = [], []
    for expert in (column, column + 1 - 2 * c):
        hit = my_ids == expert
        chosen = jnp.any(hit, axis=2)
        weights.append(jnp.sum(jnp.where(hit, my_weights, 0.0), axis=2).reshape(rows))
        rank = jnp.cumsum(chosen.astype(jnp.int32), axis=1) - 1
        slot = jnp.where(chosen, rank + most * jnp.arange(NB, dtype=jnp.int32)[:, None], -1)
        spots.append(slot.reshape(rows))
    cap = NB * most
    pick = [(jnp.arange(cap, dtype=jnp.int32)[:, None] == s[None, :]).astype(BF) for s in spots]
    picked = [dot(p, resid).astype(BF) for p in pick]
    own_rows, other_rows = ring4_gather(picked[0], picked[1], x_shift)

    shared_hidden = swiglu(
        resid,
        jnp.concatenate([shared_gate, other_held[0]], axis=1),
        jnp.concatenate([shared_up, other_held[1]], axis=1),
    )
    both_down = jnp.concatenate([shared_down, other_held[2]], axis=0)

    outs = []
    for group, (w_gate, w_up, w_down) in zip((own_rows, other_rows), (held[3:], other_held[3:])):
        expert_hidden = swiglu(jnp.concatenate(group, axis=0), w_gate, w_up)
        out = dot(expert_hidden, w_down).astype(BF)
        outs.append([out[i * cap : (i + 1) * cap] for i in range(NX)])
    routed = ring4_reduce(outs[0], outs[1], x_shift)

    scatter = []
    for s, w in zip(spots, weights):
        scatter.append(jnp.where(s[:, None] == jnp.arange(cap, dtype=jnp.int32)[None, :], w[:, None], 0.0))
    scatter = jnp.concatenate(scatter, axis=1)
    coarse = scatter.astype(BF)
    fine = (scatter - coarse.astype(F32)).astype(BF)
    routed = jnp.concatenate(routed, axis=0).astype(BF)
    left = jnp.concatenate([coarse, fine, shared_hidden], axis=1)
    right = jnp.concatenate([routed, routed, both_down], axis=0)
    term = dot(left, right).astype(BF)
    final = reduce_rows(term)
    return (own_resid.astype(F32) + final).astype(BF)


def solution(mesh):
    return jax.shard_map(
        body,
        mesh=mesh,
        in_specs=(
            P("dp", None),
            P("dp"),
            P(),
            P(None, "mp"),
            P(None, "mp"),
            P("mp", None),
            P(None, "mp"),
            P(None, "mp"),
            P("mp", None),
            P("mp", None, "dp"),
            P("mp", None, "dp"),
            P("mp", "dp", None),
            P("dp", None),
            P("dp", None),
        ),
        out_specs=P(("dp", "mp"), None),
        check_vma=False,
    )
```

```python
import jax
import jax.numpy as jnp
from jax import lax
from jax.experimental import pallas as pl
from jax.experimental.pallas import tpu as pltpu
from jax.sharding import PartitionSpec as P

BF = jnp.bfloat16
F32 = jnp.float32
NX, NZ, NY = 4, 8, 4
NB = NZ * NY
MOST = 3
NEAR = (0, 1, 7, 6)
FAR = (5, 4, 3, 2)
HALF_BLOCKS = NB // 2
CAP = HALF_BLOCKS * MOST


def mp_perm(dz, dy, dc):
    pairs = []
    for z in range(NZ):
        for y in range(NY):
            for c in range(2):
                to = ((z + dz) % NZ) * 2 * NY + ((y + dy) % NY) * 2 + (c + dc) % 2
                pairs.append((z * 2 * NY + y * 2 + c, to))
    return pairs


def core_swap(v):
    return lax.ppermute(v, "mp", mp_perm(0, 0, 1))


def z_shift(v, s):
    return lax.ppermute(v, "mp", mp_perm(s, 0, 0))


def y_shift(v, s):
    return lax.ppermute(v, "mp", mp_perm(0, s, 0))


def x_shift(v, s):
    return lax.ppermute(v, "dp", [(i, (i + s) % NX) for i in range(NX)])


def plus(a, b):
    return (a.astype(F32) + b.astype(F32)).astype(BF)


def ring4_reduce(lo, hi, shift):
    a = shift(lo[2], 1)
    b = shift(hi[2], -1)
    c = shift(hi[1], 1)
    d = shift(lo[3], -1)
    e = shift(plus(lo[1], a), 1)
    f = shift(plus(hi[3], b), -1)
    own_lo = lo[0].astype(F32) + d.astype(F32) + e.astype(F32)
    own_hi = hi[0].astype(F32) + c.astype(F32) + f.astype(F32)
    return own_lo.astype(BF), own_hi.astype(BF)


def ring4_gather(lo, hi, shift):
    a = shift(lo, 1)
    b = shift(hi, -1)
    c = shift(hi, 1)
    d = shift(lo, -1)
    e = shift(a, 1)
    f = shift(b, -1)
    return [lo, d, e, a], [hi, b, f, c]


def reduce_rows(lo, hi):
    up_lo = z_shift(lo[4], 1)
    dn_hi = z_shift(hi[4], -1)
    up_hi = z_shift(hi[3], 1)
    dn_lo = z_shift(lo[5], -1)
    for d in (3, 2, 1):
        up_lo = z_shift(plus(lo[d], up_lo), 1)
        dn_hi = z_shift(plus(hi[NZ - d], dn_hi), -1)
        if d > 1:
            up_hi = z_shift(plus(hi[d - 1], up_hi), 1)
            dn_lo = z_shift(plus(lo[NZ + 1 - d], dn_lo), -1)
    mid_lo = lo[0].astype(F32) + up_lo.astype(F32) + dn_lo.astype(F32)
    mid_hi = hi[0].astype(F32) + up_hi.astype(F32) + dn_hi.astype(F32)
    two = y_shift(mid_hi[:16].astype(BF), 2)
    one = y_shift(mid_lo[16:].astype(BF), 1)
    three = y_shift(mid_hi[16:].astype(BF), 3)
    return mid_lo[:16] + two.astype(F32) + one.astype(F32) + three.astype(F32)


def gather_rows(own):
    two = y_shift(own, 2)
    three = y_shift(own, 1)
    one = y_shift(own, -1)
    lo = {0: jnp.concatenate([own, one], axis=0)}
    hi = {0: jnp.concatenate([two, three], axis=0)}
    up_lo, up_hi, dn_lo, dn_hi = lo[0], hi[0], lo[0], hi[0]
    for d in (1, 2, 3):
        up_lo = lo[NZ - d] = z_shift(up_lo, 1)
        dn_hi = hi[d] = z_shift(dn_hi, -1)
        up_hi = hi[NZ - d] = z_shift(up_hi, 1)
        dn_lo = lo[d] = z_shift(dn_lo, -1)
    lo[4] = z_shift(up_lo, 1)
    hi[4] = z_shift(dn_hi, -1)
    return lo, hi


def dot(a, b):
    return jnp.dot(a, b, preferred_element_type=F32)


def dot_t(a, b):
    return lax.dot_general(a, b, (((1,), (1,)), ((), ())), preferred_element_type=F32)


def swiglu_t(rows, gate_t, up_t):
    gate = dot_t(rows, gate_t)
    up = dot_t(rows, up_t)
    return (gate / (1.0 + jnp.exp(-gate)) * up).astype(BF)


def dense_kernel(index_ref, *refs):
    tokens = refs[:HALF_BLOCKS]
    lookup, bias, gate_a, up_a, down_a, gate_b, up_b, down_b = refs[HALF_BLOCKS : HALF_BLOCKS + 8]
    own, *pieces = refs[HALF_BLOCKS + 8 :]
    rows = jnp.concatenate([t[0] for t in tokens], axis=0)
    stream = (rows.astype(F32) + dot(lookup[...], bias[...])).astype(BF)
    own[...] = stream[:16]
    hidden_a = swiglu_t(stream, gate_a[...], up_a[...])
    hidden_b = swiglu_t(stream, gate_b[...], up_b[...])
    out = (dot(hidden_a, down_a[...]) + dot(hidden_b, down_b[...])).astype(BF)
    for k, piece in enumerate(pieces):
        piece[...] = out[k * 32 : (k + 1) * 32]


def dense(index, tokens, lookup, bias, weights):
    d_model = tokens.shape[2]
    full = lambda a: pl.BlockSpec(a.shape, lambda i, index: (0, 0))
    block = lambda k: pl.BlockSpec((1, 16, d_model), lambda i, index: (index[k], 0, 0))
    out_shape = [jax.ShapeDtypeStruct((16, d_model), BF)] + [jax.ShapeDtypeStruct((32, d_model), BF)] * 8
    return pl.pallas_call(
        dense_kernel,
        out_shape=out_shape,
        grid_spec=pltpu.PrefetchScalarGridSpec(
            num_scalar_prefetch=1,
            grid=(1,),
            in_specs=[block(k) for k in range(HALF_BLOCKS)] + [full(a) for a in (lookup, bias, *weights)],
            out_specs=[full(a) for a in out_shape],
        ),
        name="dense",
    )(index, *([tokens] * HALF_BLOCKS), lookup, bias, *weights)


def pick_kernel(pick, *refs):
    rows = jnp.concatenate([r[...] for r in refs[:8]], axis=0)
    out = dot(pick[...], rows).astype(BF)
    refs[8][...] = out[:CAP]
    refs[9][...] = out[CAP:]


def pick_rows(pick, pieces):
    shape = jax.ShapeDtypeStruct((CAP, pieces[0].shape[1]), BF)
    return pl.pallas_call(pick_kernel, out_shape=[shape, shape], name="pick")(pick, *pieces)


def shared_kernel(gate_a, up_a, gate_b, up_b, *refs):
    rows = jnp.concatenate([r[...] for r in refs[:8]], axis=0)
    refs[8][...] = swiglu_t(rows, gate_a[...], up_a[...])
    refs[9][...] = swiglu_t(rows, gate_b[...], up_b[...])


def shared(weights, pieces):
    shape = jax.ShapeDtypeStruct((HALF_BLOCKS * 16, weights[0].shape[0]), BF)
    return pl.pallas_call(shared_kernel, out_shape=[shape, shape], name="shared")(*weights, *pieces)


def expert_kernel(gate, up, down, *refs):
    rows = jnp.concatenate([r[...] for r in refs[:NX]], axis=0)
    out = dot(swiglu_t(rows, gate[...], up[...]), down[...]).astype(BF)
    for k in range(NX):
        refs[NX + k][...] = out[k * CAP : (k + 1) * CAP]


def expert(weights, pieces):
    shape = jax.ShapeDtypeStruct(pieces[0].shape, BF)
    return pl.pallas_call(expert_kernel, out_shape=[shape] * NX, name="expert")(*weights, *pieces)


def combine_kernel(coarse, fine, own, other, hidden_a, hidden_b, down_a, down_b, *pieces):
    routed = jnp.concatenate([own[...], other[...]], axis=0)
    out = dot(coarse[...], routed) + dot(fine[...], routed)
    out = (out + dot(hidden_a[...], down_a[...]) + dot(hidden_b[...], down_b[...])).astype(BF)
    for k, piece in enumerate(pieces):
        piece[...] = out[k * 32 : (k + 1) * 32]


def combine(coarse, fine, own, other, hidden, downs):
    shape = jax.ShapeDtypeStruct((32, own.shape[1]), BF)
    return pl.pallas_call(combine_kernel, out_shape=[shape] * 8, name="combine")(coarse, fine, own, other, *hidden, *downs)


def by_z(near, far):
    lo, hi = {}, {}
    for order, pieces in ((NEAR, near), (FAR, far)):
        for k, d in enumerate(order):
            lo[d], hi[d] = pieces[2 * k], pieces[2 * k + 1]
    return lo, hi


def body(
    tokens,
    domain_ids,
    domain_bias,
    dense_gate,
    dense_up,
    dense_down,
    shared_gate,
    shared_up,
    shared_down,
    expert_gate,
    expert_up,
    expert_down,
    expert_ids,
    route_weights,
):
    column = lax.axis_index("mp")
    z, y, c = column // (2 * NY), (column // 2) % NY, column % 2
    d_model = tokens.shape[1]
    dz = jnp.array(NEAR + FAR, jnp.int32)[:, None]
    dy = jnp.arange(NY, dtype=jnp.int32)[None, :]
    blocks = (((z + dz) % NZ) * 2 * NY + ((y + dy) % NY) * 2 + c).reshape(NB)
    rows = NB * 16
    half = rows // 2

    dense_own = (dense_gate.T, dense_up.T, dense_down)
    dense_other = tuple(core_swap(w) for w in dense_own)
    held = (shared_gate.T, shared_up.T, shared_down, expert_gate[0].T, expert_up[0].T, expert_down[0])
    later, dense_other = lax.optimization_barrier((held, dense_other))
    other_held = tuple(core_swap(w) for w in later)

    my_domains = jnp.take(domain_ids.reshape(2 * NB, 16), blocks, axis=0).reshape(rows)
    my_ids = jnp.take(expert_ids.reshape(2 * NB, 16, -1), blocks, axis=0)
    my_weights = jnp.take(route_weights.reshape(2 * NB, 16, -1), blocks, axis=0)
    lookup = (my_domains[:, None] == jnp.arange(domain_bias.shape[0], dtype=jnp.int32)[None, :]).astype(BF)

    token_blocks = tokens.reshape(2 * NB, 16, d_model)
    weights = dense_own + dense_other
    _, *far = dense(blocks[HALF_BLOCKS:], token_blocks, lookup[half:], domain_bias, weights)
    own_stream, *near = dense(blocks[:HALF_BLOCKS], token_blocks, lookup[:half], domain_bias, weights)
    total = reduce_rows(*by_z(near, far))
    own_resid = (own_stream.astype(F32) + total).astype(BF)
    lo, hi = gather_rows(own_resid)
    near = [v for d in NEAR for v in (lo[d], hi[d])]
    far = [v for d in FAR for v in (lo[d], hi[d])]

    spots, coefs = [], []
    for name in (column, column + 1 - 2 * c):
        hit = my_ids == name
        chosen = jnp.any(hit, axis=2)
        coefs.append(jnp.sum(jnp.where(hit, my_weights, 0.0), axis=2).reshape(2, half))
        rank = jnp.cumsum(chosen.astype(jnp.int32), axis=1) - 1
        first = MOST * (jnp.arange(NB, dtype=jnp.int32) % HALF_BLOCKS)[:, None]
        spots.append(jnp.where(chosen, rank + first, -1).reshape(2, half))
    slots = jnp.arange(CAP, dtype=jnp.int32)
    picks, coarses, fines = [], [], []
    for h in range(2):
        picks.append(jnp.concatenate([(slots[:, None] == s[h][None, :]).astype(BF) for s in spots], axis=0))
        place = [jnp.where(s[h][:, None] == slots[None, :], w[h][:, None], 0.0) for s, w in zip(spots, coefs)]
        place = jnp.concatenate(place, axis=1)
        coarses.append(place.astype(BF))
        fines.append((place - coarses[h].astype(F32)).astype(BF))

    expert_weights = (held[3:], other_held[3:])
    shared_weights = (held[0], held[1], other_held[0], other_held[1])
    shared_downs = (held[2], other_held[2])
    routed, hidden = [], []
    for h, pieces in enumerate((near, far)):
        own_rows, other_rows = ring4_gather(*pick_rows(picks[h], pieces), x_shift)
        hidden.append(shared(shared_weights, pieces))
        outs = [expert(w, group) for w, group in zip(expert_weights, (own_rows, other_rows))]
        routed.append(ring4_reduce(outs[0], outs[1], x_shift))
    terms = [combine(coarses[h], fines[h], *routed[h], hidden[h], shared_downs) for h in range(2)]
    final = reduce_rows(*by_z(*terms))
    return (own_resid.astype(F32) + final).astype(BF)


def solution(mesh):
    return jax.shard_map(
        body,
        mesh=mesh,
        in_specs=(
            P("dp", None),
            P("dp"),
            P(),
            P(None, "mp"),
            P(None, "mp"),
            P("mp", None),
            P(None, "mp"),
            P(None, "mp"),
            P("mp", None),
            P("mp", None, "dp"),
            P("mp", None, "dp"),
            P("mp", "dp", None),
            P("dp", None),
            P("dp", None),
        ),
        out_specs=P(("dp", "mp"), None),
        check_vma=False,
    )
```

```python
import jax
import jax.numpy as jnp
from jax import lax
from jax.experimental import pallas as pl
from jax.experimental.pallas import tpu as pltpu
from jax.sharding import PartitionSpec as P

BF = jnp.bfloat16
F32 = jnp.float32
NX, NZ, NY = 4, 8, 4
NB = NZ * NY
MOST = 3
CHUNK = NZ * 16
SLOTS = NZ * MOST


def mp_perm(dy, dc):
    pairs = []
    for z in range(NZ):
        for y in range(NY):
            for c in range(2):
                to = z * 2 * NY + ((y + dy) % NY) * 2 + (c + dc) % 2
                pairs.append((z * 2 * NY + y * 2 + c, to))
    return pairs


def core_swap(v):
    return lax.ppermute(v, "mp", mp_perm(0, 1))


def y_shift(v, s):
    return lax.ppermute(v, "mp", mp_perm(s, 0))


def x_shift(v, s):
    return lax.ppermute(v, "dp", [(i, (i + s) % NX) for i in range(NX)])


def z_exchange(v):
    groups = [[z * 2 * NY + k for z in range(NZ)] for k in range(2 * NY)]
    return lax.all_to_all(v, "mp", 0, 0, axis_index_groups=groups, tiled=True)


def plus(a, b):
    return (a.astype(F32) + b.astype(F32)).astype(BF)


def ring4_reduce(lo, hi, shift):
    a = shift(lo[2], 1)
    b = shift(hi[2], -1)
    c = shift(hi[1], 1)
    d = shift(lo[3], -1)
    e = shift(plus(lo[1], a), 1)
    f = shift(plus(hi[3], b), -1)
    return [lo[0], d, e], [hi[0], c, f]


def total_of(parts):
    return sum(v.astype(F32) for v in parts)


def ring4_gather_in_turn(lo, hi, shift):
    a = shift(lo, 1)
    d = shift(lo, -1)
    b = shift(hi, -1)
    later, a = lax.optimization_barrier((hi, a))
    e = shift(a, 1)
    c = shift(later, 1)
    f = shift(b, -1)
    return [lo, d, e, a], [hi, b, f, c]


def y_direct(pieces):
    got = {NY - s: y_shift(pieces[s], s) for s in (2, 1, 3)}
    return [pieces[0]] + [got[s] for s in range(1, NY)]


def z_reduce(mid):
    back = z_exchange(mid.reshape(NZ, 16, mid.shape[1]))
    return jnp.sum(back.astype(F32), axis=0)


def z_gather(own):
    return z_exchange(jnp.broadcast_to(own[None], (NZ, *own.shape))).reshape(CHUNK, own.shape[1])


def dot(a, b):
    return jnp.dot(a, b, preferred_element_type=F32)


def swiglu(rows, w_gate, w_up):
    gate = dot(rows, w_gate)
    up = dot(rows, w_up)
    return (gate / (1.0 + jnp.exp(-gate)) * up).astype(BF)


def swiglu_t(rows, gate_t, up_t):
    by_rows = (((1,), (1,)), ((), ()))
    gate = lax.dot_general(rows, gate_t, by_rows, preferred_element_type=F32)
    up = lax.dot_general(rows, up_t, by_rows, preferred_element_type=F32)
    return (gate / (1.0 + jnp.exp(-gate)) * up).astype(BF)


def dot_l(a, b):
    return lax.dot_general(a, b, (((0,), (0,)), ((), ())), preferred_element_type=F32)


def cut(out, pieces):
    size = pieces[0].shape[0]
    for k, piece in enumerate(pieces):
        piece[...] = out[k * size : (k + 1) * size]


def call(kernel, name, count, rows, *operands):
    shape = jax.ShapeDtypeStruct((rows, operands[-1].shape[1]), BF)
    return list(pl.pallas_call(kernel, out_shape=[shape] * count, name=name)(*operands))


def down_kernel(y_ref, hidden_a, hidden_b, down_a, down_b, *pieces):
    for k in range(NY):
        chunk = pl.ds(pl.multiple_of(((y_ref[0] + k) % NY) * CHUNK, CHUNK), CHUNK)
        out = dot_l(hidden_a[:, chunk], down_a[...]) + dot_l(hidden_b[:, chunk], down_b[...])
        cut(out.astype(BF), pieces[2 * k : 2 * k + 2])


def down(y, *operands):
    shape = jax.ShapeDtypeStruct((CHUNK // 2, operands[-1].shape[1]), BF)
    specs = [pl.BlockSpec(memory_space=pltpu.SMEM)] + [pl.BlockSpec(memory_space=pltpu.VMEM)] * len(operands)
    return list(
        pl.pallas_call(down_kernel, out_shape=[shape] * (2 * NY), in_specs=specs, name="down")(y.reshape(1), *operands)
    )


def expert_kernel(gate, up, down, *refs):
    rows = jnp.concatenate([r[...] for r in refs[:NX]], axis=0)
    cut(dot(swiglu_t(rows, gate[...], up[...]), down[...]).astype(BF), refs[NX:])


def pick_kernel(pick, rows, *pieces):
    cut(dot(pick[...], rows[...]).astype(BF), pieces)


def split_kernel(*refs):
    *pieces, own, other = refs
    for k, piece in enumerate(pieces):
        own[k * SLOTS : (k + 1) * SLOTS] = piece[:SLOTS]
        other[k * SLOTS : (k + 1) * SLOTS] = piece[SLOTS:]


def join_kernel(*refs):
    *parts, a, b, c, d = refs
    sums = []
    for k in range(2):
        x, y, z = parts[3 * k : 3 * k + 3]
        sums.append((x[...].astype(F32) + y[...].astype(F32) + z[...].astype(F32)).astype(BF))
    for k, piece in enumerate((a, b, c, d)):
        for part, v in enumerate(sums):
            piece[part * SLOTS : (part + 1) * SLOTS] = v[k * SLOTS : (k + 1) * SLOTS]


def combine_kernel(coarse, fine, a, b, c, d, s0, s1, s2, s3, out):
    rows = jnp.concatenate([a[...], b[...], c[...], d[...]], axis=0)
    shared = s0[...].astype(F32) + s1[...].astype(F32) + s2[...].astype(F32) + s3[...].astype(F32)
    out[...] = (shared + dot(coarse[...], rows) + dot(fine[...], rows)).astype(BF)


def body(
    tokens,
    domain_ids,
    domain_bias,
    dense_gate,
    dense_up,
    dense_down,
    shared_gate,
    shared_up,
    shared_down,
    expert_gate,
    expert_up,
    expert_down,
    expert_ids,
    route_weights,
):
    column = lax.axis_index("mp")
    y, c = (column // 2) % NY, column % 2
    d_model = tokens.shape[1]
    zs = jnp.arange(NZ, dtype=jnp.int32)
    rows = NB * 16

    def of_core(v):
        v = lax.dynamic_slice_in_dim(v.reshape(NZ, NY, 2, 16, *v.shape[1:]), c, 1, 2)[:, :, 0]
        return jnp.swapaxes(v, 0, 1).reshape(rows, *v.shape[3:])

    dense_own = (dense_gate, dense_up, dense_down)
    dense_other = tuple(core_swap(w) for w in dense_own)
    held = (shared_gate, shared_up, shared_down, expert_gate[0], expert_up[0], expert_down[0])

    def stream_of(toks, domains):
        lookup = (domains[:, None] == jnp.arange(domain_bias.shape[0], dtype=jnp.int32)[None, :]).astype(BF)
        return (toks.astype(F32) + dot(lookup, domain_bias)).astype(BF)

    stream = stream_of(of_core(tokens), of_core(domain_ids))

    hidden = [swiglu(stream, *dense_own[:2]).T, swiglu(stream, *dense_other[:2]).T]
    parts = down(y, *hidden, dense_own[2], dense_other[2])
    (expert_ids, route_weights, domain_ids), parts[4] = lax.optimization_barrier(
        ((expert_ids, route_weights, domain_ids), parts[4])
    )
    mid = [total_of(v) for v in ring4_reduce(parts[0::2], parts[1::2], y_shift)]
    mid = jnp.concatenate(mid, axis=0).astype(BF)

    own_tokens = lax.dynamic_slice_in_dim(tokens, column * 16, 16, 0)
    own_stream = stream_of(own_tokens, lax.dynamic_slice_in_dim(domain_ids, column * 16, 16, 0))

    z = column // (2 * NY)
    mine = (zs * 2 * NY + y * 2 + c).reshape(NZ)
    my_ids = jnp.take(expert_ids.reshape(2 * NB, 16, -1), mine, axis=0)
    my_weights = jnp.take(route_weights.reshape(2 * NB, 16, -1), mine, axis=0)
    base = z * 2 * NY + ((y + jnp.arange(NY, dtype=jnp.int32)) % NY) * 2
    names = jnp.stack([base + c, base + 1 - c], axis=1).reshape(2 * NY)
    hit = my_ids[None] == names[:, None, None, None]
    chosen = jnp.any(hit, axis=3)
    coef = jnp.sum(jnp.where(hit, my_weights[None], 0.0), axis=3).reshape(2 * NY, CHUNK)
    rank = jnp.cumsum(chosen.astype(jnp.int32), axis=2) - 1
    spot = jnp.where(chosen, rank + MOST * jnp.arange(NZ, dtype=jnp.int32)[None, :, None], -1).reshape(2 * NY, CHUNK)
    match = spot[:, None, :] == jnp.arange(SLOTS, dtype=jnp.int32)[None, :, None]
    pick = match.reshape(2 * NY * SLOTS, CHUNK).astype(BF)
    place = jnp.where(match, coef[:, None, :], 0.0).reshape(2 * NY * SLOTS, CHUNK).T
    coarse = place.astype(BF)
    fine = (place - coarse.astype(F32)).astype(BF)

    mid, own_stream, pick, coarse, fine = lax.optimization_barrier((mid, own_stream, pick, coarse, fine))
    own_resid = (own_stream.astype(F32) + z_reduce(mid)).astype(BF)
    block = z_gather(own_resid)

    sent = call(pick_kernel, "pick", NY, 2 * SLOTS, pick, block)
    arrived = y_direct(sent)
    own_rows, other_rows = call(split_kernel, "split", 2, NY * SLOTS, *arrived)
    (block, held), own_rows = lax.optimization_barrier(((block, held), own_rows))
    other_held = tuple(core_swap(w) for w in held)
    gathered = ring4_gather_in_turn(own_rows, other_rows, x_shift)

    blocks_y = y_direct([block] * NY)
    gate = jnp.concatenate([held[0], other_held[0]], axis=1)
    up = jnp.concatenate([held[1], other_held[1]], axis=1)
    shared_down_all = jnp.concatenate([held[2], other_held[2]], axis=0)
    shared = [dot(swiglu(v, gate, up), shared_down_all).astype(BF) for v in blocks_y]
    shared = y_direct(shared)

    size = NY * SLOTS
    outs = []
    for group, (w_gate, w_up, w_down) in zip(gathered, (held[3:], other_held[3:])):
        outs.append(call(expert_kernel, "expert", NX, size, w_gate.T, w_up.T, w_down, *group))
    routed = ring4_reduce(outs[0], outs[1], x_shift)
    back = y_direct(call(join_kernel, "join", NY, 2 * SLOTS, *routed[0], *routed[1]))
    (term,) = call(combine_kernel, "combine", 1, CHUNK, coarse, fine, *back, *shared)
    return (own_resid.astype(F32) + z_reduce(term)).astype(BF)


def solution(mesh):
    return jax.shard_map(
        body,
        mesh=mesh,
        in_specs=(
            P("dp", None),
            P("dp"),
            P(),
            P(None, "mp"),
            P(None, "mp"),
            P("mp", None),
            P(None, "mp"),
            P(None, "mp"),
            P("mp", None),
            P("mp", None, "dp"),
            P("mp", None, "dp"),
            P("mp", "dp", None),
            P("dp", None),
            P("dp", None),
        ),
        out_specs=P(("dp", "mp"), None),
        check_vma=False,
    )
```

```python
import jax
import jax.numpy as jnp
from jax import lax
from jax.experimental import pallas as pl
from jax.experimental.pallas import tpu as pltpu
from jax.sharding import PartitionSpec as P

BF = jnp.bfloat16
F32 = jnp.float32
NX, NZ, NY = 4, 8, 4
NB = NZ * NY
MOST = 3
CHUNK = NZ * 16
SLOTS = NZ * MOST


def mp_perm(dy, dc):
    pairs = []
    for z in range(NZ):
        for y in range(NY):
            for c in range(2):
                to = z * 2 * NY + ((y + dy) % NY) * 2 + (c + dc) % 2
                pairs.append((z * 2 * NY + y * 2 + c, to))
    return pairs


def core_swap(v):
    return lax.ppermute(v, "mp", mp_perm(0, 1))


def y_shift(v, s):
    return lax.ppermute(v, "mp", mp_perm(s, 0))


def x_shift(v, s):
    return lax.ppermute(v, "dp", [(i, (i + s) % NX) for i in range(NX)])


def z_exchange(v):
    groups = [[z * 2 * NY + k for z in range(NZ)] for k in range(2 * NY)]
    return lax.all_to_all(v, "mp", 0, 0, axis_index_groups=groups, tiled=True)


def plus(a, b):
    return (a.astype(F32) + b.astype(F32)).astype(BF)


def ring4_reduce(lo, hi, shift):
    a = shift(lo[2], 1)
    b = shift(hi[2], -1)
    c = shift(hi[1], 1)
    d = shift(lo[3], -1)
    e = shift(plus(lo[1], a), 1)
    f = shift(plus(hi[3], b), -1)
    return [lo[0], d, e], [hi[0], c, f]


def total_of(parts):
    return sum(v.astype(F32) for v in parts)


def ring4_gather_in_turn(lo, hi, shift):
    a = shift(lo, 1)
    d = shift(lo, -1)
    b = shift(hi, -1)
    later, a = lax.optimization_barrier((hi, a))
    e = shift(a, 1)
    c = shift(later, 1)
    f = shift(b, -1)
    return [lo, d, e, a], [hi, b, f, c]


def y_direct(pieces):
    got = {NY - s: y_shift(pieces[s], s) for s in (2, 1, 3)}
    return [pieces[0]] + [got[s] for s in range(1, NY)]


def z_reduce(mid):
    back = z_exchange(mid.reshape(NZ, 16, mid.shape[1]))
    return jnp.sum(back.astype(F32), axis=0)


def z_gather(own):
    return z_exchange(jnp.broadcast_to(own[None], (NZ, *own.shape))).reshape(CHUNK, own.shape[1])


def dot(a, b):
    return jnp.dot(a, b, preferred_element_type=F32)


def swiglu(rows, w_gate, w_up):
    gate = dot(rows, w_gate)
    up = dot(rows, w_up)
    return (gate / (1.0 + jnp.exp(-gate)) * up).astype(BF)


def swiglu_t(rows, gate_t, up_t):
    by_rows = (((1,), (1,)), ((), ()))
    gate = lax.dot_general(rows, gate_t, by_rows, preferred_element_type=F32)
    up = lax.dot_general(rows, up_t, by_rows, preferred_element_type=F32)
    return (gate / (1.0 + jnp.exp(-gate)) * up).astype(BF)


def dot_l(a, b):
    return lax.dot_general(a, b, (((0,), (0,)), ((), ())), preferred_element_type=F32)


def cut(out, pieces):
    size = pieces[0].shape[0]
    for k, piece in enumerate(pieces):
        piece[...] = out[k * size : (k + 1) * size]


def call(kernel, name, count, rows, *operands):
    shape = pltpu.VMEM((rows, operands[-1].shape[1]), BF)
    return list(pl.pallas_call(kernel, out_shape=[shape] * count, name=name)(*operands))


def down_kernel(y_ref, hidden_a, hidden_b, down_a, down_b, *pieces):
    for k in range(NY):
        chunk = pl.ds(pl.multiple_of(((y_ref[0] + k) % NY) * CHUNK, CHUNK), CHUNK)
        out = dot_l(hidden_a[:, chunk], down_a[...]) + dot_l(hidden_b[:, chunk], down_b[...])
        cut(out.astype(BF), pieces[2 * k : 2 * k + 2])


def down(y, *operands):
    shape = pltpu.VMEM((CHUNK // 2, operands[-1].shape[1]), BF)
    specs = [pl.BlockSpec(memory_space=pltpu.SMEM)] + [pl.BlockSpec(memory_space=pltpu.VMEM)] * len(operands)
    return list(
        pl.pallas_call(down_kernel, out_shape=[shape] * (2 * NY), in_specs=specs, name="down")(y.reshape(1), *operands)
    )


def expert_kernel(gate, up, down, *refs):
    rows = jnp.concatenate([r[...] for r in refs[:NX]], axis=0)
    cut(dot(swiglu_t(rows, gate[...], up[...]), down[...]).astype(BF), refs[NX:])


def pick_kernel(pick, rows, *pieces):
    cut(dot(pick[...], rows[...]).astype(BF), pieces)


def split_kernel(*refs):
    *pieces, own, other = refs
    for k, piece in enumerate(pieces):
        own[k * SLOTS : (k + 1) * SLOTS] = piece[:SLOTS]
        other[k * SLOTS : (k + 1) * SLOTS] = piece[SLOTS:]


def join_kernel(*refs):
    *parts, a, b, c, d = refs
    sums = []
    for k in range(2):
        x, y, z = parts[3 * k : 3 * k + 3]
        sums.append((x[...].astype(F32) + y[...].astype(F32) + z[...].astype(F32)).astype(BF))
    for k, piece in enumerate((a, b, c, d)):
        for part, v in enumerate(sums):
            piece[part * SLOTS : (part + 1) * SLOTS] = v[k * SLOTS : (k + 1) * SLOTS]


def combine_kernel(coarse, fine, a, b, c, d, s0, s1, s2, s3, out):
    rows = jnp.concatenate([a[...], b[...], c[...], d[...]], axis=0)
    shared = s0[...].astype(F32) + s1[...].astype(F32) + s2[...].astype(F32) + s3[...].astype(F32)
    out[...] = (shared + dot(coarse[...], rows) + dot(fine[...], rows)).astype(BF)


def body(
    tokens,
    domain_ids,
    domain_bias,
    dense_gate,
    dense_up,
    dense_down,
    shared_gate,
    shared_up,
    shared_down,
    expert_gate,
    expert_up,
    expert_down,
    expert_ids,
    route_weights,
):
    column = lax.axis_index("mp")
    y, c = (column // 2) % NY, column % 2
    d_model = tokens.shape[1]
    zs = jnp.arange(NZ, dtype=jnp.int32)
    rows = NB * 16

    def of_core(v):
        v = lax.dynamic_slice_in_dim(v.reshape(NZ, NY, 2, 16, *v.shape[1:]), c, 1, 2)[:, :, 0]
        return jnp.swapaxes(v, 0, 1).reshape(rows, *v.shape[3:])

    dense_own = (dense_gate, dense_up, dense_down)
    dense_other = tuple(core_swap(w) for w in dense_own)
    held = (shared_gate, shared_up, shared_down, expert_gate[0], expert_up[0], expert_down[0])

    def stream_of(toks, domains):
        lookup = (domains[:, None] == jnp.arange(domain_bias.shape[0], dtype=jnp.int32)[None, :]).astype(BF)
        return (toks.astype(F32) + dot(lookup, domain_bias)).astype(BF)

    stream = stream_of(of_core(tokens), of_core(domain_ids))

    hidden = [swiglu(stream, *dense_own[:2]).T, swiglu(stream, *dense_other[:2]).T]
    parts = down(y, *hidden, dense_own[2], dense_other[2])
    (expert_ids, route_weights, domain_ids), parts[4] = lax.optimization_barrier(
        ((expert_ids, route_weights, domain_ids), parts[4])
    )
    mid = [total_of(v) for v in ring4_reduce(parts[0::2], parts[1::2], y_shift)]
    mid = jnp.concatenate(mid, axis=0).astype(BF)

    own_tokens = lax.dynamic_slice_in_dim(tokens, column * 16, 16, 0)
    own_stream = stream_of(own_tokens, lax.dynamic_slice_in_dim(domain_ids, column * 16, 16, 0))

    z = column // (2 * NY)
    mine = (zs * 2 * NY + y * 2 + c).reshape(NZ)
    my_ids = jnp.take(expert_ids.reshape(2 * NB, 16, -1), mine, axis=0)
    my_weights = jnp.take(route_weights.reshape(2 * NB, 16, -1), mine, axis=0)
    base = z * 2 * NY + ((y + jnp.arange(NY, dtype=jnp.int32)) % NY) * 2
    names = jnp.stack([base + c, base + 1 - c], axis=1).reshape(2 * NY)
    hit = my_ids[None] == names[:, None, None, None]
    chosen = jnp.any(hit, axis=3)
    coef = jnp.sum(jnp.where(hit, my_weights[None], 0.0), axis=3).reshape(2 * NY, CHUNK)
    rank = jnp.cumsum(chosen.astype(jnp.int32), axis=2) - 1
    spot = jnp.where(chosen, rank + MOST * jnp.arange(NZ, dtype=jnp.int32)[None, :, None], -1).reshape(2 * NY, CHUNK)
    match = spot[:, None, :] == jnp.arange(SLOTS, dtype=jnp.int32)[None, :, None]
    pick = match.reshape(2 * NY * SLOTS, CHUNK).astype(BF)
    place = jnp.where(match, coef[:, None, :], 0.0).reshape(2 * NY * SLOTS, CHUNK).T
    coarse = place.astype(BF)
    fine = (place - coarse.astype(F32)).astype(BF)

    mid, own_stream, pick, coarse, fine = lax.optimization_barrier((mid, own_stream, pick, coarse, fine))
    own_resid = (own_stream.astype(F32) + z_reduce(mid)).astype(BF)
    block = z_gather(own_resid)

    sent = call(pick_kernel, "pick", NY, 2 * SLOTS, pick, block)
    arrived = y_direct(sent)
    own_rows, other_rows = call(split_kernel, "split", 2, NY * SLOTS, *arrived)
    (block, held), own_rows = lax.optimization_barrier(((block, held), own_rows))
    other_held = tuple(core_swap(w) for w in held)
    gathered = ring4_gather_in_turn(own_rows, other_rows, x_shift)

    blocks_y = y_direct([block] * NY)
    gate = jnp.concatenate([held[0], other_held[0]], axis=1)
    up = jnp.concatenate([held[1], other_held[1]], axis=1)
    shared_down_all = jnp.concatenate([held[2], other_held[2]], axis=0)
    shared = [dot(swiglu(v, gate, up), shared_down_all).astype(BF) for v in blocks_y]
    shared = y_direct(shared)

    size = NY * SLOTS
    outs = []
    for group, (w_gate, w_up, w_down) in zip(gathered, (held[3:], other_held[3:])):
        outs.append(call(expert_kernel, "expert", NX, size, w_gate.T, w_up.T, w_down, *group))
    routed = ring4_reduce(outs[0], outs[1], x_shift)
    back = y_direct(call(join_kernel, "join", NY, 2 * SLOTS, *routed[0], *routed[1]))
    (term,) = call(combine_kernel, "combine", 1, CHUNK, coarse, fine, *back, *shared)
    return (own_resid.astype(F32) + z_reduce(term)).astype(BF)


def solution(mesh):
    return jax.shard_map(
        body,
        mesh=mesh,
        in_specs=(
            P("dp", None),
            P("dp"),
            P(),
            P(None, "mp"),
            P(None, "mp"),
            P("mp", None),
            P(None, "mp"),
            P(None, "mp"),
            P("mp", None),
            P("mp", None, "dp"),
            P("mp", None, "dp"),
            P("mp", "dp", None),
            P("dp", None),
            P("dp", None),
        ),
        out_specs=P(("dp", "mp"), None),
        check_vma=False,
    )
```
